32 devices in a mesh: pb: 4 (over x, core), ga: 8 (over z, y).
Axes of the slice: x: 2, y: 2, z: 4, core: 2. Of those that a mesh axis runs over, the one named last changes fastest.
Arguments:
- queries: bfloat16 [8192, 512], P(('pb', 'ga')), may hold values from -4 to 4
- gallery: bfloat16 [12288, 512], P('ga'), may hold values from -1 to 1
- positives: int32 [8192, 4], P('pb'), may hold values from 0 to 12287, as said below
- cutoffs: int32 [4], replicated, may hold values from 1 to 385
Outputs:
- query_grad: float32 [8192, 512], P(('pb', 'ga'))
- gallery_grad: float32 [12288, 512], P(('ga', 'pb'))
The draws below stay inside these ranges and needn't reach their ends.
Inputs may be any that keep to these rules, and one draw needn't show every extreme that they name: `positives`: indices of a query may repeat.
All inputs are finite; a program needn't handle non-finite values.
Results may differ from the reference program's by a relative error of at most 0.0043.
Values may be sent and summed in bfloat16 or wider, within the bound.
A program may use at most 64 MiB of HBM per device.

```python
import jax
import jax.numpy as jnp
from jax import lax

D = 512
NPOS = 4
NCUT = 4
Q = 8192
G = 12288


def common_draw(key):
    base = jax.random.fold_in(key, 911)
    key_gallery, key_pos, key_strength, key_noise = jax.random.split(base, 4)
    positives = jax.random.randint(key_pos, (Q, NPOS), 0, G, dtype=jnp.int32)
    gallery = jnp.clip(jax.random.normal(key_gallery, (G, D), jnp.float32), -4.0, 4.0) * D ** (-0.5)
    gallery = gallery.astype(jnp.bfloat16).astype(jnp.float32)
    strength = jnp.exp(jax.random.uniform(key_strength, (Q, 1), jnp.float32, jnp.log(0.2), jnp.log(0.7)))
    summed = jnp.sum(gallery[positives], axis=1)
    noise = jax.random.normal(key_noise, (Q, D), jnp.float32) * D ** (-0.5)
    queries = jnp.clip(strength * summed + noise, -4.0, 4.0)
    return (gallery, positives, queries)


def draw_gallery(key, part):
    return common_draw(key)[0].astype(jnp.bfloat16)


def draw_positives(key, part):
    return common_draw(key)[1]


def draw_queries(key, part):
    return common_draw(key)[2].astype(jnp.bfloat16)


def touch_ends(array, key, least, high):
    longest = array.shape.index(max(array.shape))
    spots = []
    for shift in (0, 1):
        where = [jax.random.randint(jax.random.fold_in(key, axis), (), 0, length) for axis, length in enumerate(array.shape)]
        where[longest] = (where[longest] + shift) % array.shape[longest]
        spots.append(tuple(where))
    return array.at[spots[0]].set(least).at[spots[1]].set(high)


def setup_inputs(seed: int = 0) -> dict:
    seeds = jax.random.split(jax.random.key(seed), 5)
    queries = draw_queries(jax.random.fold_in(seeds[4], 71), 0)
    gallery = draw_gallery(jax.random.fold_in(seeds[4], 71), 0)
    positives = draw_positives(jax.random.fold_in(seeds[4], 71), 0)
    cutoffs = touch_ends(jax.random.randint(seeds[3], (NCUT,), 1, G // 32 + 2), jax.random.fold_in(seeds[3], 1), 1, (G // 32 + 2) - 1).astype(jnp.int32)
    return {"queries": queries, "gallery": gallery, "positives": positives, "cutoffs": cutoffs}


TEMP = 0.05
SHARP = 4.0


def reference(queries, gallery, positives, cutoffs):
    block_rows = min(512, Q)
    blocks = Q // block_rows
    cut_values = cutoffs.astype(jnp.float32)

    def handle(gallery_acc, pieces):
        query_block, pos_block = pieces
        scores = jnp.dot(query_block, gallery.T, preferred_element_type=jnp.float32)
        anchor = jnp.take_along_axis(scores, pos_block, axis=1)
        counted = []
        slopes = []
        for member in range(NPOS):
            squash = jax.nn.sigmoid((scores - anchor[:, member:member + 1]) / TEMP)
            counted.append(0.5 + jnp.sum(squash, axis=1))
            slopes.append(jnp.sum(squash * (1.0 - squash), axis=1) / TEMP)
        rank_total = jnp.stack(counted, axis=1)
        slope_total = jnp.stack(slopes, axis=1)
        recall = jax.nn.sigmoid(SHARP * (cut_values - rank_total[:, :, None]) / cut_values)
        weight_rank = jnp.sum(recall * (1.0 - recall) * SHARP / cut_values, axis=-1) / (NPOS * NCUT)
        weight = jnp.zeros(scores.shape, jnp.float32)
        for member in range(NPOS):
            squash = jax.nn.sigmoid((scores - anchor[:, member:member + 1]) / TEMP)
            weight = weight + weight_rank[:, member:member + 1] * squash * (1.0 - squash) / TEMP
        row_index = jnp.arange(block_rows, dtype=jnp.int32)[:, None]
        weight = weight.at[row_index, pos_block].add(-weight_rank * slope_total)
        dscore = weight.astype(jnp.bfloat16)
        query_part = jnp.dot(dscore, gallery, preferred_element_type=jnp.float32)
        gallery_acc = gallery_acc + jnp.dot(dscore.T, query_block, preferred_element_type=jnp.float32)
        return gallery_acc, query_part

    start_acc = jnp.zeros((G, D), jnp.float32)
    gallery_grad, query_parts = lax.scan(
        handle, start_acc,
        (queries.reshape(blocks, block_rows, D), positives.reshape(blocks, block_rows, NPOS)))
    return query_parts.reshape(Q, D), gallery_grad
```

```python
import functools

import jax
import jax.numpy as jnp
from jax import lax
from jax.experimental import pallas as pl
from jax.experimental.pallas import tpu as pltpu
from jax.sharding import PartitionSpec as P

TEMP = 0.05
SHARP = 4.0
LANES = 128
GROUP = 16
MESH = pl.DeviceIdType.MESH


def kernel(
    n, npb, cut_ref, q_ref, g_ref, idx_ref, qout_ref, gout_ref,
    qs, sc, dsc, pos_in, rank_in, stage, cols, qp_out, qp_in,
    gal_f, gal_b, ga_in, gb_out, gb_in,
    q_send, q_recv, pos_send, pos_recv, rank_send, rank_recv, qp_send, qp_recv,
    ga_send, ga_recv, gb_send, gb_recv,
):
    rows, width = q_ref.shape
    gal = g_ref.shape[0]
    members = idx_ref.shape[1]
    cuts = cut_ref.shape[0]
    chunks = gal // LANES
    nx = npb // 2
    cols_x = gal // nx
    half = cols_x // 2
    per_x = cols_x // LANES
    me = lax.axis_index("ga")
    mp = lax.axis_index("pb")
    my_x = mp // 2
    core = lax.rem(mp, 2)
    partner = mp + 1 - 2 * core
    groups = rows // GROUP

    barrier = pltpu.get_barrier_semaphore()
    for p in range(1, n):
        pl.semaphore_signal(barrier, inc=1, device_id={"ga": lax.rem(me + p, n)}, device_id_type=MESH)
    for p in range(1, npb):
        pl.semaphore_signal(barrier, inc=1, device_id={"pb": lax.rem(mp + p, npb)}, device_id_type=MESH)
    pl.semaphore_wait(barrier, n - 1 + npb - 1)

    def query_copy(p):
        return pltpu.make_async_remote_copy(
            src_ref=q_ref, dst_ref=qs.at[p], send_sem=q_send.at[p], recv_sem=q_recv.at[p],
            device_id={"ga": lax.rem(me + p, n)}, device_id_type=MESH)

    for p in range(1, n):
        query_copy(p).start()
    qs[0] = q_ref[...]

    lane = lax.broadcasted_iota(jnp.int32, (GROUP, LANES), 1)

    def spread(column):
        return jnp.broadcast_to(column, (GROUP, LANES))

    def keys_of(r, i):
        owner = lax.rem(me - r + n, n)
        start = pl.multiple_of(owner * rows + i * GROUP, GROUP)
        local = idx_ref[pl.ds(start, GROUP), :] - me * gal
        return [spread(local[:, m:m + 1]) - lane for m in range(members)]

    def exchange(buf, r, send, recv):
        @pl.loop(1, n)
        def _(p):
            pltpu.make_async_remote_copy(
                src_ref=buf.at[r, 0], dst_ref=buf.at[lax.rem(r + p, n), p],
                send_sem=send.at[r], recv_sem=recv.at[lax.rem(r + p, n)],
                device_id={"ga": lax.rem(me + p, n)}, device_id_type=MESH).start()

    def exchange_wait(buf, r, send, recv):
        return pltpu.make_async_remote_copy(
            src_ref=buf.at[r, pl.ds(1, n - 1)], dst_ref=buf.at[r, pl.ds(1, n - 1)],
            send_sem=send.at[r], recv_sem=recv.at[r],
            device_id={"ga": lax.rem(me + 1, n)}, device_id_type=MESH)

    def to_lanes(values):
        out = jnp.zeros((GROUP, LANES), jnp.float32)
        for k, value in enumerate(values):
            out = jnp.where(lane == k, spread(value), out)
        return out

    @pl.loop(0, n)
    def _(r):
        @pl.when(r > 0)
        def _():
            query_copy(r).wait_recv()

        sc[r] = lax.dot_general(
            qs[r], g_ref[...], (((1,), (1,)), ((), ())), preferred_element_type=jnp.float32)

        @pl.loop(0, groups)
        def _(i):
            at = pl.ds(pl.multiple_of(i * GROUP, GROUP), GROUP)
            keys = keys_of(r, i)
            picked = [jnp.zeros((GROUP, LANES), jnp.float32) for _ in range(members)]
            for c in range(chunks):
                s = sc[r, at, c * LANES:(c + 1) * LANES] * (0.5 / TEMP)
                sc[r, at, c * LANES:(c + 1) * LANES] = s
                picked = [jnp.where(keys[m] == c * LANES, s, picked[m]) for m in range(members)]
            stage[at, :] = to_lanes([jnp.sum(x, axis=1, keepdims=True) for x in picked])

        pos_in[r, 0] = jnp.transpose(stage[...])[:8]
        exchange(pos_in, r, pos_send, pos_recv)

    @pl.loop(0, n)
    def _(r):
        exchange_wait(pos_in, r, pos_send, pos_recv).wait_recv()
        anchor = jnp.sum(pos_in[r], axis=0)
        cols[r, 0] = jnp.transpose(anchor)

        @pl.loop(0, groups)
        def _(i):
            at = pl.ds(pl.multiple_of(i * GROUP, GROUP), GROUP)
            anchors = cols[r, 0, at, :]
            a = [spread(anchors[:, m:m + 1]) for m in range(members)]
            total = [jnp.zeros((GROUP, LANES), jnp.float32) for _ in range(members)]
            square = [jnp.zeros((GROUP, LANES), jnp.float32) for _ in range(members)]
            for c in range(chunks):
                s = sc[r, at, c * LANES:(c + 1) * LANES]
                for m in range(members):
                    u = 1.0 + jnp.tanh(s - a[m])
                    total[m] = total[m] + u
                    square[m] = square[m] + u * u
            sums = [jnp.sum(x, axis=1, keepdims=True) for x in total]
            slopes = [
                jnp.sum(2.0 * x - y, axis=1, keepdims=True) for x, y in zip(total, square)]
            stage[at, :] = to_lanes(sums + slopes)

        rank_in[r, 0] = jnp.transpose(stage[...])[:2 * members]
        exchange(rank_in, r, rank_send, rank_recv)

    @pl.loop(0, n)
    def _(r):
        exchange_wait(rank_in, r, rank_send, rank_recv).wait_recv()
        both = jnp.sum(rank_in[r], axis=0)
        rank = 0.5 + 0.5 * both[:members]
        slope = both[members:] * (0.25 / TEMP)
        wr = jnp.zeros(rank.shape, jnp.float32)
        for c in range(cuts):
            kv = jnp.full(rank.shape, cut_ref[c], jnp.int32).astype(jnp.float32)
            e = jnp.exp(-jnp.abs(SHARP * (kv - rank) / kv))
            wr = wr + e / ((1.0 + e) * (1.0 + e)) * SHARP / kv
        wr = wr / (members * cuts)
        cols[r, 1] = jnp.transpose(jnp.concatenate([wr * (0.25 / TEMP), wr * slope], axis=0))

        @pl.loop(0, groups)
        def _(i):
            at = pl.ds(pl.multiple_of(i * GROUP, GROUP), GROUP)
            at_all = pl.ds(pl.multiple_of(r * rows + i * GROUP, GROUP), GROUP)
            keys = keys_of(r, i)
            anchors = cols[r, 0, at, :]
            weights = cols[r, 1, at, :]
            a = [spread(anchors[:, m:m + 1]) for m in range(members)]
            w = [spread(weights[:, m:m + 1]) for m in range(members)]
            spike = [spread(weights[:, members + m:members + m + 1]) for m in range(members)]
            base = sum(w[1:], w[0])
            for c in range(chunks):
                s = sc[r, at, c * LANES:(c + 1) * LANES]
                d = base
                for m in range(members):
                    t = jnp.tanh(s - a[m])
                    d = d - w[m] * (t * t)
                for m in range(members):
                    d = d - jnp.where(keys[m] == c * LANES, spike[m], 0.0)
                k = c % per_x
                dsc[c // per_x, at_all, k * LANES:(k + 1) * LANES] = d.astype(jnp.bfloat16)

        part = jnp.zeros((rows, width), jnp.float32)
        block = pl.ds(pl.multiple_of(r * rows, rows), rows)
        for x in range(nx):
            part = part + jnp.dot(
                dsc[x, block, :], g_ref[x * cols_x:(x + 1) * cols_x, :],
                preferred_element_type=jnp.float32)

        @pl.when(r == 0)
        def _():
            qout_ref[...] = part

        @pl.when(r > 0)
        def _():
            qp_out[r] = part.astype(jnp.bfloat16)
            pltpu.make_async_remote_copy(
                src_ref=qp_out.at[r], dst_ref=qp_in.at[r], send_sem=qp_send.at[r], recv_sem=qp_recv.at[r],
                device_id={"ga": lax.rem(me - r + n, n)}, device_id_type=MESH).start()

    def pair_copy(x):
        return pltpu.make_async_remote_copy(
            src_ref=gal_b.at[x, 1 - core], dst_ref=ga_in.at[x], send_sem=ga_send.at[x], recv_sem=ga_recv.at[x],
            device_id={"pb": partner}, device_id_type=MESH)

    def chip_copy(k):
        return pltpu.make_async_remote_copy(
            src_ref=gb_out.at[k], dst_ref=gb_in.at[k], send_sem=gb_send.at[k], recv_sem=gb_recv.at[k],
            device_id={"pb": lax.rem(my_x + 1 + k, nx) * 2 + core}, device_id_type=MESH)

    qall = qs[...].reshape(n * rows, width)
    for k in range(nx):
        x = lax.rem(my_x + 1 + k, nx)
        for h in range(2):
            res = lax.dot_general(
                dsc[x, :, h * half:(h + 1) * half], qall, (((0,), (0,)), ((), ())),
                preferred_element_type=jnp.float32)
            gal_f[x, h] = res
            gal_b[x, h] = res.astype(jnp.bfloat16)
        pair_copy(x).start()

    for k in range(nx - 1):
        x = lax.rem(my_x + 1 + k, nx)
        pair_copy(x).wait_recv()
        gb_out[k] = (gal_f[x, core] + ga_in[x].astype(jnp.float32)).astype(jnp.bfloat16)
        chip_copy(k).start()
    pair_copy(my_x).wait_recv()
    gout_ref[...] = gal_f[my_x, core] + ga_in[my_x].astype(jnp.float32)

    @pl.loop(1, n)
    def _(r):
        pltpu.make_async_remote_copy(
            src_ref=qp_out.at[r], dst_ref=qp_in.at[r], send_sem=qp_send.at[r], recv_sem=qp_recv.at[r],
            device_id={"ga": lax.rem(me - r + n, n)}, device_id_type=MESH).wait()
        qout_ref[...] += qp_in[r].astype(jnp.float32)
        query_copy(r).wait_send()

    for k in range(nx - 1):
        chip_copy(k).wait()
        gout_ref[...] += gb_in[k].astype(jnp.float32)

    @pl.loop(0, n)
    def _(r):
        exchange_wait(pos_in, r, pos_send, pos_recv).wait_send()
        exchange_wait(rank_in, r, rank_send, rank_recv).wait_send()

    @pl.loop(0, nx)
    def _(x):
        pair_copy(x).wait_send()


def shards(n, npb, queries, gallery, positives, cutoffs):
    rows, width = queries.shape
    gal = gallery.shape[0]
    members = positives.shape[1]
    nx = npb // 2
    half = gal // npb
    dma = pltpu.SemaphoreType.DMA
    vmem = pl.BlockSpec(memory_space=pltpu.VMEM)
    f32, bf16 = jnp.float32, jnp.bfloat16
    return pl.pallas_call(
        functools.partial(kernel, n, npb),
        out_shape=(
            jax.ShapeDtypeStruct((rows, width), f32),
            jax.ShapeDtypeStruct((half, width), f32),
        ),
        in_specs=[pl.BlockSpec(memory_space=pltpu.SMEM), vmem, vmem, vmem],
        out_specs=(vmem, vmem),
        scratch_shapes=[
            pltpu.VMEM((n, rows, width), bf16),
            pltpu.VMEM((n, rows, gal), f32),
            pltpu.VMEM((nx, n * rows, gal // nx), bf16),
            pltpu.VMEM((n, n, 8, rows), f32),
            pltpu.VMEM((n, n, 2 * members, rows), f32),
            pltpu.VMEM((rows, LANES), f32),
            pltpu.VMEM((n, 2, rows, 8), f32),
            pltpu.VMEM((n, rows, width), bf16),
            pltpu.VMEM((n, rows, width), bf16),
            pltpu.VMEM((nx, 2, half, width), f32),
            pltpu.VMEM((nx, 2, half, width), bf16),
            pltpu.VMEM((nx, half, width), bf16),
            pltpu.VMEM((max(nx - 1, 1), half, width), bf16),
            pltpu.VMEM((max(nx - 1, 1), half, width), bf16),
            dma((n,)), dma((n,)), dma((n,)), dma((n,)), dma((n,)), dma((n,)), dma((n,)), dma((n,)),
            dma((nx,)), dma((nx,)), dma((nx,)), dma((nx,)),
        ],
        compiler_params=pltpu.CompilerParams(
            collective_id=0, has_side_effects=True, vmem_limit_bytes=62 * 1024 * 1024),
    )(cutoffs, queries, gallery, positives)


def solution(mesh):
    placed = (P(("pb", "ga"), None), P("ga", None), P("pb", None), P())
    return jax.shard_map(
        functools.partial(shards, mesh.shape["ga"], mesh.shape["pb"]),
        mesh=mesh,
        in_specs=placed,
        out_specs=(P(("pb", "ga"), None), P(("ga", "pb"), None)),
        check_vma=False,
    )
```

```python
import functools

import jax
import jax.numpy as jnp
from jax import lax
from jax.experimental import pallas as pl
from jax.experimental.pallas import tpu as pltpu
from jax.sharding import PartitionSpec as P

TEMP = 0.05
SHARP = 4.0
LANES = 128
GROUP = 16
MESH = pl.DeviceIdType.MESH


def kernel(
    n, npb, cut_ref, q_ref, g_ref, idx_ref, qout_ref, gout_ref,
    qs, sc, dsc, pos_in, rank_in, stage, cols, qp_out, qp_in,
    own_part, z_out, z_in, gal_f, gal_b, ga_in, gb_out, gb_in,
    q_send, q_recv, pos_send, pos_recv, rank_send, rank_recv, y_send, y_recv, z_send, z_recv,
    ga_send, ga_recv, gb_send, gb_recv,
):
    rows, width = q_ref.shape
    gal = g_ref.shape[0]
    members = idx_ref.shape[1]
    cuts = cut_ref.shape[0]
    chunks = gal // LANES
    nx = npb // 2
    cols_x = gal // nx
    half = cols_x // 2
    per_x = cols_x // LANES
    me = lax.axis_index("ga")
    mp = lax.axis_index("pb")
    my_x = mp // 2
    core = lax.rem(mp, 2)
    partner = mp + 1 - 2 * core
    groups = rows // GROUP
    depth = n // 2
    z = me // 2
    y = lax.rem(me, 2)
    across = z * 2 + 1 - y
    hr = rows // 2

    barrier = pltpu.get_barrier_semaphore()
    for p in range(1, n):
        pl.semaphore_signal(barrier, inc=1, device_id={"ga": lax.rem(me + p, n)}, device_id_type=MESH)
    for p in range(1, npb):
        pl.semaphore_signal(barrier, inc=1, device_id={"pb": lax.rem(mp + p, npb)}, device_id_type=MESH)
    pl.semaphore_wait(barrier, n - 1 + npb - 1)

    def hop(source, o, h, d, target):
        return pltpu.make_async_remote_copy(
            src_ref=source, dst_ref=qs.at[o, pl.ds(h * hr, hr)], send_sem=q_send.at[o, h, d],
            recv_sem=q_recv.at[o, h], device_id={"ga": target}, device_id_type=MESH)

    def hops(zo, yo, h, act, own=False):
        o = zo * 2 + yo
        source = q_ref.at[pl.ds(h * hr, hr)] if own else qs.at[o, pl.ds(h * hr, hr)]
        along = (h == 1) | (yo == y)

        @pl.when(along & (zo <= z) & (z < depth - 1))
        def _():
            act(hop(source, o, h, 0, lax.rem(me + 2, n)))

        @pl.when(along & (zo >= z) & (z > 0))
        def _():
            act(hop(source, o, h, 1, lax.rem(me - 2 + n, n)))

        @pl.when((yo == y) & ((h == 0) | (zo == z)))
        def _():
            act(hop(source, o, h, 2, across))

    def candidate(j):
        k = j // 2
        step = (k + 1) // 2
        zo = jnp.where(lax.rem(k, 2) == 1, z - step, z + step)
        yo = jnp.where(lax.rem(j, 2) == 0, y, 1 - y)
        return zo, yo, (zo >= 0) & (zo < depth)

    for h in range(2):
        hops(z, y, h, lambda c: c.start(), own=True)
    qs[me] = q_ref[...]

    lane = lax.broadcasted_iota(jnp.int32, (GROUP, LANES), 1)

    def spread(column):
        return jnp.broadcast_to(column, (GROUP, LANES))

    def keys_of(owner, i):
        start = pl.multiple_of(owner * rows + i * GROUP, GROUP)
        local = idx_ref[pl.ds(start, GROUP), :] - me * gal
        return [spread(local[:, m:m + 1]) - lane for m in range(members)]

    def exchange(buf, r, send, recv):
        @pl.loop(1, n)
        def _(p):
            pltpu.make_async_remote_copy(
                src_ref=buf.at[r, 0], dst_ref=buf.at[r, p],
                send_sem=send.at[r], recv_sem=recv.at[r],
                device_id={"ga": lax.rem(me + p, n)}, device_id_type=MESH).start()

    def exchange_wait(buf, r, send, recv):
        return pltpu.make_async_remote_copy(
            src_ref=buf.at[r, pl.ds(1, n - 1)], dst_ref=buf.at[r, pl.ds(1, n - 1)],
            send_sem=send.at[r], recv_sem=recv.at[r],
            device_id={"ga": lax.rem(me + 1, n)}, device_id_type=MESH)

    def to_lanes(values):
        out = jnp.zeros((GROUP, LANES), jnp.float32)
        for k, value in enumerate(values):
            out = jnp.where(lane == k, spread(value), out)
        return out

    def score_block(r):
        sc[r] = lax.dot_general(
            qs[r], g_ref[...], (((1,), (1,)), ((), ())), preferred_element_type=jnp.float32)

        @pl.loop(0, groups)
        def _(i):
            at = pl.ds(pl.multiple_of(i * GROUP, GROUP), GROUP)
            keys = keys_of(r, i)
            picked = [jnp.zeros((GROUP, LANES), jnp.float32) for _ in range(members)]
            for c in range(chunks):
                s = sc[r, at, c * LANES:(c + 1) * LANES] * (0.5 / TEMP)
                sc[r, at, c * LANES:(c + 1) * LANES] = s
                picked = [jnp.where(keys[m] == c * LANES, s, picked[m]) for m in range(members)]
            stage[at, :] = to_lanes([jnp.sum(x, axis=1, keepdims=True) for x in picked])

        pos_in[r, 0] = jnp.transpose(stage[...])[:members]
        exchange(pos_in, r, pos_send, pos_recv)

    @pl.loop(0, 2 * (2 * depth - 1))
    def _(j):
        zo, yo, valid = candidate(j)

        @pl.when(valid)
        def _():
            @pl.when(j > 0)
            def _():
                for h in range(2):
                    hop(qs.at[zo * 2 + yo, pl.ds(h * hr, hr)], zo * 2 + yo, h, 0, across).wait_recv()
                    hops(zo, yo, h, lambda c: c.start())

            score_block(zo * 2 + yo)

    @pl.loop(0, n)
    def _(r):
        exchange_wait(pos_in, r, pos_send, pos_recv).wait_recv()
        anchor = jnp.sum(pos_in[r], axis=0)
        cols[r, 0] = jnp.transpose(jnp.concatenate([anchor, anchor], axis=0))

        @pl.loop(0, groups)
        def _(i):
            at = pl.ds(pl.multiple_of(i * GROUP, GROUP), GROUP)
            anchors = cols[r, 0, at, :]
            a = [spread(anchors[:, m:m + 1]) for m in range(members)]
            total = [jnp.zeros((GROUP, LANES), jnp.float32) for _ in range(members)]
            square = [jnp.zeros((GROUP, LANES), jnp.float32) for _ in range(members)]
            for c in range(chunks):
                s = sc[r, at, c * LANES:(c + 1) * LANES]
                for m in range(members):
                    u = 1.0 + jnp.tanh(s - a[m])
                    total[m] = total[m] + u
                    square[m] = square[m] + u * u
            sums = [jnp.sum(x, axis=1, keepdims=True) for x in total]
            slopes = [
                jnp.sum(2.0 * x - y, axis=1, keepdims=True) for x, y in zip(total, square)]
            stage[at, :] = to_lanes(sums + slopes)

        rank_in[r, 0] = jnp.transpose(stage[...])[:2 * members]
        exchange(rank_in, r, rank_send, rank_recv)

    def fold_copy(zo):
        return pltpu.make_async_remote_copy(
            src_ref=qp_out.at[zo], dst_ref=qp_in.at[zo], send_sem=y_send.at[zo], recv_sem=y_recv.at[zo],
            device_id={"ga": across}, device_id_type=MESH)

    def home_copy(k):
        return pltpu.make_async_remote_copy(
            src_ref=z_out.at[k], dst_ref=z_in.at[k], send_sem=z_send.at[k], recv_sem=z_recv.at[k],
            device_id={"ga": lax.rem(z + k, depth) * 2 + y}, device_id_type=MESH)

    @pl.loop(0, n)
    def _(t):
        step = t // 2
        first = lax.rem(t, 2) == 0
        zo = lax.rem(z + 1 + step, depth)
        r = zo * 2 + jnp.where(first, 1 - y, y)
        exchange_wait(rank_in, r, rank_send, rank_recv).wait_recv()
        both = jnp.sum(rank_in[r], axis=0)
        rank = 0.5 + 0.5 * both[:members]
        slope = both[members:] * (0.25 / TEMP)
        wr = jnp.zeros(rank.shape, jnp.float32)
        for c in range(cuts):
            kv = jnp.full(rank.shape, cut_ref[c], jnp.int32).astype(jnp.float32)
            e = jnp.exp(-jnp.abs(SHARP * (kv - rank) / kv))
            wr = wr + e / ((1.0 + e) * (1.0 + e)) * SHARP / kv
        wr = wr / (members * cuts)
        cols[r, 1] = jnp.transpose(jnp.concatenate([wr * (0.25 / TEMP), wr * slope], axis=0))

        @pl.loop(0, groups)
        def _(i):
            at = pl.ds(pl.multiple_of(i * GROUP, GROUP), GROUP)
            at_all = pl.ds(pl.multiple_of(r * rows + i * GROUP, GROUP), GROUP)
            keys = keys_of(r, i)
            anchors = cols[r, 0, at, :]
            weights = cols[r, 1, at, :]
            a = [spread(anchors[:, m:m + 1]) for m in range(members)]
            w = [spread(weights[:, m:m + 1]) for m in range(members)]
            spike = [spread(weights[:, members + m:members + m + 1]) for m in range(members)]
            base = sum(w[1:], w[0])
            for c in range(chunks):
                s = sc[r, at, c * LANES:(c + 1) * LANES]
                d = base
                for m in range(members):
                    t = jnp.tanh(s - a[m])
                    d = d - w[m] * (t * t)
                for m in range(members):
                    d = d - jnp.where(keys[m] == c * LANES, spike[m], 0.0)
                k = c % per_x
                dsc[c // per_x, at_all, k * LANES:(k + 1) * LANES] = d.astype(jnp.bfloat16)

        part = jnp.zeros((rows, width), jnp.float32)
        block = pl.ds(pl.multiple_of(r * rows, rows), rows)
        for x in range(nx):
            part = part + jnp.dot(
                dsc[x, block, :], g_ref[x * cols_x:(x + 1) * cols_x, :],
                preferred_element_type=jnp.float32)

        @pl.when(first)
        def _():
            qp_out[zo] = part.astype(jnp.bfloat16)
            fold_copy(zo).start()

        @pl.when(jnp.logical_not(first))
        def _():
            own_part[zo] = part

            @pl.when(step > 0)
            def _():
                zf = lax.rem(z + step, depth)
                fold_copy(zf).wait_recv()
                z_out[step] = (own_part[zf] + qp_in[zf].astype(jnp.float32)).astype(jnp.bfloat16)
                home_copy(step).start()

    def pair_copy(x):
        return pltpu.make_async_remote_copy(
            src_ref=gal_b.at[x, 1 - core], dst_ref=ga_in.at[x], send_sem=ga_send.at[x], recv_sem=ga_recv.at[x],
            device_id={"pb": partner}, device_id_type=MESH)

    def chip_copy(k):
        return pltpu.make_async_remote_copy(
            src_ref=gb_out.at[k], dst_ref=gb_in.at[k], send_sem=gb_send.at[k], recv_sem=gb_recv.at[k],
            device_id={"pb": lax.rem(my_x + 1 + k, nx) * 2 + core}, device_id_type=MESH)

    qall = qs[...].reshape(n * rows, width)
    for k in range(nx):
        x = lax.rem(my_x + 1 + k, nx)
        for h in range(2):
            res = lax.dot_general(
                dsc[x, :, h * half:(h + 1) * half], qall, (((0,), (0,)), ((), ())),
                preferred_element_type=jnp.float32)
            gal_f[x, h] = res
            gal_b[x, h] = res.astype(jnp.bfloat16)
        pair_copy(x).start()

    for k in range(nx - 1):
        x = lax.rem(my_x + 1 + k, nx)
        pair_copy(x).wait_recv()
        gb_out[k] = (gal_f[x, core] + ga_in[x].astype(jnp.float32)).astype(jnp.bfloat16)
        chip_copy(k).start()
    pair_copy(my_x).wait_recv()
    gout_ref[...] = gal_f[my_x, core] + ga_in[my_x].astype(jnp.float32)

    fold_copy(z).wait_recv()
    qout_ref[...] = own_part[z] + qp_in[z].astype(jnp.float32)

    @pl.loop(1, depth)
    def _(k):
        home_copy(k).wait()
        qout_ref[...] += z_in[k].astype(jnp.float32)

    @pl.loop(0, depth)
    def _(k):
        fold_copy(k).wait_send()

    @pl.loop(0, 2 * (2 * depth - 1))
    def _(j):
        zo, yo, valid = candidate(j)

        @pl.when(valid)
        def _():
            for h in range(2):
                hops(zo, yo, h, lambda c: c.wait_send())

    for k in range(nx - 1):
        chip_copy(k).wait()
        gout_ref[...] += gb_in[k].astype(jnp.float32)

    @pl.loop(0, n)
    def _(r):
        exchange_wait(pos_in, r, pos_send, pos_recv).wait_send()
        exchange_wait(rank_in, r, rank_send, rank_recv).wait_send()

    @pl.loop(0, nx)
    def _(x):
        pair_copy(x).wait_send()


def shards(n, npb, queries, gallery, positives, cutoffs):
    rows, width = queries.shape
    gal = gallery.shape[0]
    members = positives.shape[1]
    nx = npb // 2
    half = gal // npb
    dma = pltpu.SemaphoreType.DMA
    vmem = pl.BlockSpec(memory_space=pltpu.VMEM)
    f32, bf16 = jnp.float32, jnp.bfloat16
    return pl.pallas_call(
        functools.partial(kernel, n, npb),
        out_shape=(
            jax.ShapeDtypeStruct((rows, width), f32),
            jax.ShapeDtypeStruct((half, width), f32),
        ),
        in_specs=[pl.BlockSpec(memory_space=pltpu.SMEM), vmem, vmem, vmem],
        out_specs=(vmem, vmem),
        scratch_shapes=[
            pltpu.VMEM((n, rows, width), bf16),
            pltpu.VMEM((n, rows, gal), f32),
            pltpu.VMEM((nx, n * rows, gal // nx), bf16),
            pltpu.VMEM((n, n, members, rows), f32),
            pltpu.VMEM((n, n, 2 * members, rows), f32),
            pltpu.VMEM((rows, LANES), f32),
            pltpu.VMEM((n, 2, rows, 8), f32),
            pltpu.VMEM((n // 2, rows, width), bf16),
            pltpu.VMEM((n // 2, rows, width), bf16),
            pltpu.VMEM((n // 2, rows, width), f32),
            pltpu.VMEM((n // 2, rows, width), bf16),
            pltpu.VMEM((n // 2, rows, width), bf16),
            pltpu.VMEM((nx, 2, half, width), f32),
            pltpu.VMEM((nx, 2, half, width), bf16),
            pltpu.VMEM((nx, half, width), bf16),
            pltpu.VMEM((max(nx - 1, 1), half, width), bf16),
            pltpu.VMEM((max(nx - 1, 1), half, width), bf16),
            dma((n, 2, 3)), dma((n, 2)), dma((n,)), dma((n,)), dma((n,)), dma((n,)),
            dma((n // 2,)), dma((n // 2,)), dma((n // 2,)), dma((n // 2,)),
            dma((nx,)), dma((nx,)), dma((nx,)), dma((nx,)),
        ],
        compiler_params=pltpu.CompilerParams(
            collective_id=0, has_side_effects=True, vmem_limit_bytes=62 * 1024 * 1024),
    )(cutoffs, queries, gallery, positives)


def solution(mesh):
    placed = (P(("pb", "ga"), None), P("ga", None), P("pb", None), P())
    return jax.shard_map(
        functools.partial(shards, mesh.shape["ga"], mesh.shape["pb"]),
        mesh=mesh,
        in_specs=placed,
        out_specs=(P(("pb", "ga"), None), P(("ga", "pb"), None)),
        check_vma=False,
    )
```

```python
import functools

import jax
import jax.numpy as jnp
from jax import lax
from jax.experimental import pallas as pl
from jax.experimental.pallas import tpu as pltpu
from jax.sharding import PartitionSpec as P

TEMP = 0.05
SHARP = 4.0
LANES = 128
GROUP = 32
MESH = pl.DeviceIdType.MESH


def kernel(
    n, npb, cut_ref, q_ref, g_ref, idx_ref, qout_ref, gout_ref,
    qs, sc, dsc, pos_in, rank_in, stage, cols, qp_out, qp_in,
    own_part, z_out, z_in, gal_f, gal_b, ga_in, gb_out, gb_in,
    q_send, q_recv, pos_send, pos_recv, rank_send, rank_recv, y_send, y_recv, z_send, z_recv,
    ga_send, ga_recv, gb_send, gb_recv,
):
    rows, width = q_ref.shape
    gal = g_ref.shape[0]
    members = idx_ref.shape[1]
    cuts = cut_ref.shape[0]
    chunks = gal // LANES
    nx = npb // 2
    cols_x = gal // nx
    half = cols_x // 2
    per_x = cols_x // LANES
    me = lax.axis_index("ga")
    mp = lax.axis_index("pb")
    my_x = mp // 2
    core = lax.rem(mp, 2)
    partner = mp + 1 - 2 * core
    groups = rows // GROUP
    depth = n // 2
    z = me // 2
    y = lax.rem(me, 2)
    across = z * 2 + 1 - y
    hr = rows // 2

    barrier = pltpu.get_barrier_semaphore()
    for p in range(1, n):
        pl.semaphore_signal(barrier, inc=1, device_id={"ga": lax.rem(me + p, n)}, device_id_type=MESH)
    for p in range(1, npb):
        pl.semaphore_signal(barrier, inc=1, device_id={"pb": lax.rem(mp + p, npb)}, device_id_type=MESH)
    pl.semaphore_wait(barrier, n - 1 + npb - 1)

    def hop(source, o, h, d, target):
        return pltpu.make_async_remote_copy(
            src_ref=source, dst_ref=qs.at[o, pl.ds(h * hr, hr)], send_sem=q_send.at[o, h, d],
            recv_sem=q_recv.at[o, h], device_id={"ga": target}, device_id_type=MESH)

    def hops(zo, yo, h, act, own=False):
        o = zo * 2 + yo
        source = q_ref.at[pl.ds(h * hr, hr)] if own else qs.at[o, pl.ds(h * hr, hr)]
        along = (h == 1) | (yo == y)

        @pl.when(along & (zo <= z) & (z < depth - 1))
        def _():
            act(hop(source, o, h, 0, lax.rem(me + 2, n)))

        @pl.when(along & (zo >= z) & (z > 0))
        def _():
            act(hop(source, o, h, 1, lax.rem(me - 2 + n, n)))

        @pl.when((yo == y) & ((h == 0) | (zo == z)))
        def _():
            act(hop(source, o, h, 2, across))

    def candidate(j):
        k = j // 2
        step = (k + 1) // 2
        zo = jnp.where(lax.rem(k, 2) == 1, z - step, z + step)
        yo = jnp.where(lax.rem(j, 2) == 0, y, 1 - y)
        return zo, yo, (zo >= 0) & (zo < depth)

    for h in range(2):
        hops(z, y, h, lambda c: c.start(), own=True)
    qs[me] = q_ref[...]

    lane = lax.broadcasted_iota(jnp.int32, (GROUP, LANES), 1)

    def spread(column):
        return jnp.broadcast_to(column, (GROUP, LANES))

    def keys_of(owner, i):
        start = pl.multiple_of(owner * rows + i * GROUP, GROUP)
        local = idx_ref[pl.ds(start, GROUP), :] - me * gal
        return [spread(local[:, m:m + 1]) - lane for m in range(members)]

    def exchange(buf, r, send, recv):
        @pl.loop(1, n)
        def _(p):
            pltpu.make_async_remote_copy(
                src_ref=buf.at[r, 0], dst_ref=buf.at[r, p],
                send_sem=send.at[r], recv_sem=recv.at[r],
                device_id={"ga": lax.rem(me + p, n)}, device_id_type=MESH).start()

    def exchange_wait(buf, r, send, recv):
        return pltpu.make_async_remote_copy(
            src_ref=buf.at[r, pl.ds(1, n - 1)], dst_ref=buf.at[r, pl.ds(1, n - 1)],
            send_sem=send.at[r], recv_sem=recv.at[r],
            device_id={"ga": lax.rem(me + 1, n)}, device_id_type=MESH)

    def to_lanes(values):
        out = jnp.zeros((GROUP, LANES), jnp.float32)
        for k, value in enumerate(values):
            out = jnp.where(lane == k, spread(value), out)
        return out

    def score_block(r):
        sc[r] = lax.dot_general(
            qs[r], g_ref[...], (((1,), (1,)), ((), ())), preferred_element_type=jnp.float32)

        @pl.loop(0, groups, unroll=2)
        def _(i):
            at = pl.ds(pl.multiple_of(i * GROUP, GROUP), GROUP)
            keys = keys_of(r, i)
            picked = [jnp.zeros((GROUP, LANES), jnp.float32) for _ in range(members)]
            for c in range(chunks):
                s = sc[r, at, c * LANES:(c + 1) * LANES] * (0.5 / TEMP)
                sc[r, at, c * LANES:(c + 1) * LANES] = s
                picked = [jnp.where(keys[m] == c * LANES, s, picked[m]) for m in range(members)]
            stage[at, :] = to_lanes([jnp.sum(x, axis=1, keepdims=True) for x in picked])

        pos_in[r, 0] = jnp.transpose(stage[...])[:members]
        exchange(pos_in, r, pos_send, pos_recv)

    @pl.loop(0, 2 * (2 * depth - 1))
    def _(j):
        zo, yo, valid = candidate(j)

        @pl.when(valid)
        def _():
            @pl.when(j > 0)
            def _():
                for h in range(2):
                    hop(qs.at[zo * 2 + yo, pl.ds(h * hr, hr)], zo * 2 + yo, h, 0, across).wait_recv()
                    hops(zo, yo, h, lambda c: c.start())

            score_block(zo * 2 + yo)

    @pl.loop(0, n)
    def _(r):
        exchange_wait(pos_in, r, pos_send, pos_recv).wait_recv()
        anchor = jnp.sum(pos_in[r], axis=0)
        cols[r, 0] = jnp.transpose(jnp.concatenate([anchor, anchor], axis=0))

        @pl.loop(0, groups, unroll=2)
        def _(i):
            at = pl.ds(pl.multiple_of(i * GROUP, GROUP), GROUP)
            anchors = cols[r, 0, at, :]
            a = [spread(anchors[:, m:m + 1]) for m in range(members)]
            total = [jnp.zeros((GROUP, LANES), jnp.float32) for _ in range(members)]
            square = [jnp.zeros((GROUP, LANES), jnp.float32) for _ in range(members)]
            for c in range(chunks):
                s = sc[r, at, c * LANES:(c + 1) * LANES]
                for m in range(members):
                    t = jnp.tanh(s - a[m])
                    total[m] = total[m] + t
                    square[m] = square[m] + t * t
            sums = [jnp.sum(chunks + x, axis=1, keepdims=True) for x in total]
            slopes = [jnp.sum(chunks - x, axis=1, keepdims=True) for x in square]
            stage[at, :] = to_lanes(sums + slopes)

        rank_in[r, 0] = jnp.transpose(stage[...])[:2 * members]
        exchange(rank_in, r, rank_send, rank_recv)

    def fold_copy(zo):
        return pltpu.make_async_remote_copy(
            src_ref=qp_out.at[zo], dst_ref=qp_in.at[zo], send_sem=y_send.at[zo], recv_sem=y_recv.at[zo],
            device_id={"ga": across}, device_id_type=MESH)

    def home_copy(k):
        return pltpu.make_async_remote_copy(
            src_ref=z_out.at[k], dst_ref=z_in.at[k], send_sem=z_send.at[k], recv_sem=z_recv.at[k],
            device_id={"ga": lax.rem(z + k, depth) * 2 + y}, device_id_type=MESH)

    @pl.loop(0, n)
    def _(t):
        step = t // 2
        first = lax.rem(t, 2) == 0
        zo = lax.rem(z + 1 + step, depth)
        r = zo * 2 + jnp.where(first, 1 - y, y)
        exchange_wait(rank_in, r, rank_send, rank_recv).wait_recv()
        both = jnp.sum(rank_in[r], axis=0)
        rank = 0.5 + 0.5 * both[:members]
        slope = both[members:] * (0.25 / TEMP)
        wr = jnp.zeros(rank.shape, jnp.float32)
        for c in range(cuts):
            kv = jnp.full(rank.shape, cut_ref[c], jnp.int32).astype(jnp.float32)
            e = jnp.exp(-jnp.abs(SHARP * (kv - rank) / kv))
            wr = wr + e / ((1.0 + e) * (1.0 + e)) * SHARP / kv
        wr = wr / (members * cuts)
        cols[r, 1] = jnp.transpose(jnp.concatenate([wr * (0.25 / TEMP), wr * slope], axis=0))

        @pl.loop(0, groups, unroll=2)
        def _(i):
            at = pl.ds(pl.multiple_of(i * GROUP, GROUP), GROUP)
            at_all = pl.ds(pl.multiple_of(r * rows + i * GROUP, GROUP), GROUP)
            keys = keys_of(r, i)
            anchors = cols[r, 0, at, :]
            weights = cols[r, 1, at, :]
            a = [spread(anchors[:, m:m + 1]) for m in range(members)]
            w = [spread(weights[:, m:m + 1]) for m in range(members)]
            spike = [spread(weights[:, members + m:members + m + 1]) for m in range(members)]
            base = sum(w[1:], w[0])
            for c in range(chunks):
                s = sc[r, at, c * LANES:(c + 1) * LANES]
                d = base
                for m in range(members):
                    t = jnp.tanh(s - a[m])
                    d = d - w[m] * (t * t)
                for m in range(members):
                    d = d - jnp.where(keys[m] == c * LANES, spike[m], 0.0)
                k = c % per_x
                dsc[c // per_x, at_all, k * LANES:(k + 1) * LANES] = d.astype(jnp.bfloat16)

        part = jnp.zeros((rows, width), jnp.float32)
        block = pl.ds(pl.multiple_of(r * rows, rows), rows)
        for x in range(nx):
            part = part + jnp.dot(
                dsc[x, block, :], g_ref[x * cols_x:(x + 1) * cols_x, :],
                preferred_element_type=jnp.float32)

        @pl.when(first)
        def _():
            qp_out[zo] = part.astype(jnp.bfloat16)
            fold_copy(zo).start()

        @pl.when(jnp.logical_not(first))
        def _():
            own_part[zo] = part

            @pl.when(step > 0)
            def _():
                zf = lax.rem(z + step, depth)
                fold_copy(zf).wait_recv()
                z_out[step] = (own_part[zf] + qp_in[zf].astype(jnp.float32)).astype(jnp.bfloat16)
                home_copy(step).start()

    def pair_copy(x):
        return pltpu.make_async_remote_copy(
            src_ref=gal_b.at[x, 1 - core], dst_ref=ga_in.at[x], send_sem=ga_send.at[x], recv_sem=ga_recv.at[x],
            device_id={"pb": partner}, device_id_type=MESH)

    def chip_copy(k):
        return pltpu.make_async_remote_copy(
            src_ref=gb_out.at[k], dst_ref=gb_in.at[k], send_sem=gb_send.at[k], recv_sem=gb_recv.at[k],
            device_id={"pb": lax.rem(my_x + 1 + k, nx) * 2 + core}, device_id_type=MESH)

    qall = qs[...].reshape(n * rows, width)
    for k in range(nx):
        x = lax.rem(my_x + 1 + k, nx)
        for h in range(2):
            res = lax.dot_general(
                dsc[x, :, h * half:(h + 1) * half], qall, (((0,), (0,)), ((), ())),
                preferred_element_type=jnp.float32)
            gal_f[x, h] = res
            gal_b[x, h] = res.astype(jnp.bfloat16)
        pair_copy(x).start()

    for k in range(nx - 1):
        x = lax.rem(my_x + 1 + k, nx)
        pair_copy(x).wait_recv()
        gb_out[k] = (gal_f[x, core] + ga_in[x].astype(jnp.float32)).astype(jnp.bfloat16)
        chip_copy(k).start()
    pair_copy(my_x).wait_recv()
    gout_ref[...] = gal_f[my_x, core] + ga_in[my_x].astype(jnp.float32)

    fold_copy(z).wait_recv()
    qout_ref[...] = own_part[z] + qp_in[z].astype(jnp.float32)

    @pl.loop(1, depth)
    def _(k):
        home_copy(k).wait()
        qout_ref[...] += z_in[k].astype(jnp.float32)

    @pl.loop(0, depth)
    def _(k):
        fold_copy(k).wait_send()

    @pl.loop(0, 2 * (2 * depth - 1))
    def _(j):
        zo, yo, valid = candidate(j)

        @pl.when(valid)
        def _():
            for h in range(2):
                hops(zo, yo, h, lambda c: c.wait_send())

    for k in range(nx - 1):
        chip_copy(k).wait()
        gout_ref[...] += gb_in[k].astype(jnp.float32)

    @pl.loop(0, n)
    def _(r):
        exchange_wait(pos_in, r, pos_send, pos_recv).wait_send()
        exchange_wait(rank_in, r, rank_send, rank_recv).wait_send()

    @pl.loop(0, nx)
    def _(x):
        pair_copy(x).wait_send()


def shards(n, npb, queries, gallery, positives, cutoffs):
    rows, width = queries.shape
    gal = gallery.shape[0]
    members = positives.shape[1]
    nx = npb // 2
    half = gal // npb
    dma = pltpu.SemaphoreType.DMA
    vmem = pl.BlockSpec(memory_space=pltpu.VMEM)
    f32, bf16 = jnp.float32, jnp.bfloat16
    return pl.pallas_call(
        functools.partial(kernel, n, npb),
        out_shape=(
            jax.ShapeDtypeStruct((rows, width), f32),
            jax.ShapeDtypeStruct((half, width), f32),
        ),
        in_specs=[pl.BlockSpec(memory_space=pltpu.SMEM), vmem, vmem, vmem],
        out_specs=(vmem, vmem),
        scratch_shapes=[
            pltpu.VMEM((n, rows, width), bf16),
            pltpu.VMEM((n, rows, gal), f32),
            pltpu.VMEM((nx, n * rows, gal // nx), bf16),
            pltpu.VMEM((n, n, members, rows), f32),
            pltpu.VMEM((n, n, 2 * members, rows), f32),
            pltpu.VMEM((rows, LANES), f32),
            pltpu.VMEM((n, 2, rows, 8), f32),
            pltpu.VMEM((n // 2, rows, width), bf16),
            pltpu.VMEM((n // 2, rows, width), bf16),
            pltpu.VMEM((n // 2, rows, width), f32),
            pltpu.VMEM((n // 2, rows, width), bf16),
            pltpu.VMEM((n // 2, rows, width), bf16),
            pltpu.VMEM((nx, 2, half, width), f32),
            pltpu.VMEM((nx, 2, half, width), bf16),
            pltpu.VMEM((nx, half, width), bf16),
            pltpu.VMEM((max(nx - 1, 1), half, width), bf16),
            pltpu.VMEM((max(nx - 1, 1), half, width), bf16),
            dma((n, 2, 3)), dma((n, 2)), dma((n,)), dma((n,)), dma((n,)), dma((n,)),
            dma((n // 2,)), dma((n // 2,)), dma((n // 2,)), dma((n // 2,)),
            dma((nx,)), dma((nx,)), dma((nx,)), dma((nx,)),
        ],
        compiler_params=pltpu.CompilerParams(
            collective_id=0, has_side_effects=True, vmem_limit_bytes=62 * 1024 * 1024),
    )(cutoffs, queries, gallery, positives)


def solution(mesh):
    placed = (P(("pb", "ga"), None), P("ga", None), P("pb", None), P())
    return jax.shard_map(
        functools.partial(shards, mesh.shape["ga"], mesh.shape["pb"]),
        mesh=mesh,
        in_specs=placed,
        out_specs=(P(("pb", "ga"), None), P(("ga", "pb"), None)),
        check_vma=False,
    )
```

```python
import functools

import jax
import jax.numpy as jnp
from jax import lax
from jax.experimental import pallas as pl
from jax.experimental.pallas import tpu as pltpu
from jax.sharding import PartitionSpec as P

TEMP = 0.05
SHARP = 4.0
LANES = 128
GROUP = 32
MESH = pl.DeviceIdType.MESH


def kernel(
    n, npb, cut_ref, q_ref, g_ref, idx_ref, qout_ref, gout_ref,
    qs, sc, dsc, pos_in, rank_in, stage, cols, qp_out, qp_in,
    own_part, z_out, z_in, gal_f, gal_b, ga_in, gb_out, gb_in,
    q_send, q_recv, pos_send, pos_recv, rank_send, rank_recv, y_send, y_recv, z_send, z_recv,
    ga_send, ga_recv, gb_send, gb_recv,
):
    rows, width = q_ref.shape
    gal = g_ref.shape[0]
    members = idx_ref.shape[1]
    cuts = cut_ref.shape[0]
    chunks = gal // LANES
    nx = npb // 2
    cols_x = gal // nx
    half = cols_x // 2
    per_x = cols_x // LANES
    me = lax.axis_index("ga")
    mp = lax.axis_index("pb")
    my_x = mp // 2
    core = lax.rem(mp, 2)
    partner = mp + 1 - 2 * core
    groups = rows // GROUP
    depth = n // 2
    z = me // 2
    y = lax.rem(me, 2)
    across = z * 2 + 1 - y
    hr = rows // 2

    barrier = pltpu.get_barrier_semaphore()
    for p in range(1, n):
        pl.semaphore_signal(barrier, inc=1, device_id={"ga": lax.rem(me + p, n)}, device_id_type=MESH)
    for p in range(1, npb):
        pl.semaphore_signal(barrier, inc=1, device_id={"pb": lax.rem(mp + p, npb)}, device_id_type=MESH)
    pl.semaphore_wait(barrier, n - 1 + npb - 1)

    def hop(source, o, h, d, target):
        return pltpu.make_async_remote_copy(
            src_ref=source, dst_ref=qs.at[o, pl.ds(h * hr, hr)], send_sem=q_send.at[o, h, d],
            recv_sem=q_recv.at[o, h], device_id={"ga": target}, device_id_type=MESH)

    def hops(zo, yo, h, act, own=False):
        o = zo * 2 + yo
        source = q_ref.at[pl.ds(h * hr, hr)] if own else qs.at[o, pl.ds(h * hr, hr)]
        along = (h == 1) | (yo == y)

        @pl.when(along & (zo <= z) & (z < depth - 1))
        def _():
            act(hop(source, o, h, 0, lax.rem(me + 2, n)))

        @pl.when(along & (zo >= z) & (z > 0))
        def _():
            act(hop(source, o, h, 1, lax.rem(me - 2 + n, n)))

        @pl.when((yo == y) & ((h == 0) | (zo == z)))
        def _():
            act(hop(source, o, h, 2, across))

    def candidate(j):
        k = j // 2
        step = (k + 1) // 2
        zo = jnp.where(lax.rem(k, 2) == 1, z - step, z + step)
        yo = jnp.where(lax.rem(j, 2) == 0, y, 1 - y)
        return zo, yo, (zo >= 0) & (zo < depth)

    for h in range(2):
        hops(z, y, h, lambda c: c.start(), own=True)
    qs[me] = q_ref[...]

    lane = lax.broadcasted_iota(jnp.int32, (GROUP, LANES), 1)

    def spread(column):
        return jnp.broadcast_to(column, (GROUP, LANES))

    def keys_of(owner, i):
        start = pl.multiple_of(owner * rows + i * GROUP, GROUP)
        local = idx_ref[pl.ds(start, GROUP), :] - me * gal
        return [spread(local[:, m:m + 1]) - lane for m in range(members)]

    def exchange(buf, r, send, recv):
        @pl.loop(1, n)
        def _(p):
            pltpu.make_async_remote_copy(
                src_ref=buf.at[r, 0], dst_ref=buf.at[r, p],
                send_sem=send.at[r], recv_sem=recv.at[r],
                device_id={"ga": lax.rem(me + p, n)}, device_id_type=MESH).start()

    def exchange_wait(buf, r, send, recv):
        return pltpu.make_async_remote_copy(
            src_ref=buf.at[r, pl.ds(1, n - 1)], dst_ref=buf.at[r, pl.ds(1, n - 1)],
            send_sem=send.at[r], recv_sem=recv.at[r],
            device_id={"ga": lax.rem(me + 1, n)}, device_id_type=MESH)

    def to_lanes(values):
        out = jnp.zeros((GROUP, LANES), jnp.float32)
        for k, value in enumerate(values):
            out = jnp.where(lane == k, spread(value), out)
        return out

    def score_block(r):
        sc[r] = lax.dot_general(
            qs[r], g_ref[...], (((1,), (1,)), ((), ())), preferred_element_type=jnp.float32)

        @pl.loop(0, groups, unroll=min(groups, 4))
        def _(i):
            at = pl.ds(pl.multiple_of(i * GROUP, GROUP), GROUP)
            keys = keys_of(r, i)
            picked = [jnp.zeros((GROUP, LANES), jnp.float32) for _ in range(members)]
            for c in range(chunks):
                s = sc[r, at, c * LANES:(c + 1) * LANES] * (0.5 / TEMP)
                sc[r, at, c * LANES:(c + 1) * LANES] = s
                picked = [jnp.where(keys[m] == c * LANES, s, picked[m]) for m in range(members)]
            stage[at, :] = to_lanes([jnp.sum(x, axis=1, keepdims=True) for x in picked])

        pos_in[r, 0] = jnp.transpose(stage[...])[:members]
        exchange(pos_in, r, pos_send, pos_recv)

    @pl.loop(0, 2 * (2 * depth - 1))
    def _(j):
        zo, yo, valid = candidate(j)

        @pl.when(valid)
        def _():
            @pl.when(j > 0)
            def _():
                for h in range(2):
                    hop(qs.at[zo * 2 + yo, pl.ds(h * hr, hr)], zo * 2 + yo, h, 0, across).wait_recv()
                    hops(zo, yo, h, lambda c: c.start())

            score_block(zo * 2 + yo)

    @pl.loop(0, n)
    def _(r):
        exchange_wait(pos_in, r, pos_send, pos_recv).wait_recv()
        anchor = jnp.sum(pos_in[r], axis=0)
        cols[r, 0] = jnp.transpose(jnp.concatenate([anchor, anchor], axis=0))

        @pl.loop(0, groups, unroll=min(groups, 4))
        def _(i):
            at = pl.ds(pl.multiple_of(i * GROUP, GROUP), GROUP)
            anchors = cols[r, 0, at, :]
            a = [spread(anchors[:, m:m + 1]) for m in range(members)]
            total = [jnp.zeros((GROUP, LANES), jnp.float32) for _ in range(members)]
            square = [jnp.zeros((GROUP, LANES), jnp.float32) for _ in range(members)]
            for c in range(chunks):
                s = sc[r, at, c * LANES:(c + 1) * LANES]
                for m in range(members):
                    t = jnp.tanh(s - a[m])
                    total[m] = total[m] + t
                    square[m] = square[m] + t * t
            sums = [jnp.sum(chunks + x, axis=1, keepdims=True) for x in total]
            slopes = [jnp.sum(chunks - x, axis=1, keepdims=True) for x in square]
            stage[at, :] = to_lanes(sums + slopes)

        rank_in[r, 0] = jnp.transpose(stage[...])[:2 * members]
        exchange(rank_in, r, rank_send, rank_recv)

    def fold_copy(zo):
        return pltpu.make_async_remote_copy(
            src_ref=qp_out.at[zo], dst_ref=qp_in.at[zo], send_sem=y_send.at[zo], recv_sem=y_recv.at[zo],
            device_id={"ga": across}, device_id_type=MESH)

    def home_copy(k):
        return pltpu.make_async_remote_copy(
            src_ref=z_out.at[k], dst_ref=z_in.at[k], send_sem=z_send.at[k], recv_sem=z_recv.at[k],
            device_id={"ga": lax.rem(z + k, depth) * 2 + y}, device_id_type=MESH)

    @pl.loop(0, n)
    def _(t):
        step = t // 2
        first = lax.rem(t, 2) == 0
        zo = lax.rem(z + 1 + step, depth)
        r = zo * 2 + jnp.where(first, 1 - y, y)
        exchange_wait(rank_in, r, rank_send, rank_recv).wait_recv()
        both = jnp.sum(rank_in[r], axis=0)
        rank = 0.5 + 0.5 * both[:members]
        slope = both[members:] * (0.25 / TEMP)
        wr = jnp.zeros(rank.shape, jnp.float32)
        for c in range(cuts):
            kv = jnp.full(rank.shape, cut_ref[c], jnp.int32).astype(jnp.float32)
            e = jnp.exp(-jnp.abs(SHARP * (kv - rank) / kv))
            wr = wr + e / ((1.0 + e) * (1.0 + e)) * SHARP / kv
        wr = wr / (members * cuts)
        cols[r, 1] = jnp.transpose(jnp.concatenate([wr * (0.25 / TEMP), wr * slope], axis=0))

        @pl.loop(0, groups, unroll=min(groups, 4))
        def _(i):
            at = pl.ds(pl.multiple_of(i * GROUP, GROUP), GROUP)
            at_all = pl.ds(pl.multiple_of(r * rows + i * GROUP, GROUP), GROUP)
            keys = keys_of(r, i)
            anchors = cols[r, 0, at, :]
            weights = cols[r, 1, at, :]
            a = [spread(anchors[:, m:m + 1]) for m in range(members)]
            w = [spread(weights[:, m:m + 1]) for m in range(members)]
            spike = [spread(weights[:, members + m:members + m + 1]) for m in range(members)]
            base = sum(w[1:], w[0])
            for c in range(chunks):
                s = sc[r, at, c * LANES:(c + 1) * LANES]
                d = base
                for m in range(members):
                    t = jnp.tanh(s - a[m])
                    d = d - w[m] * (t * t)
                for m in range(members):
                    d = d - jnp.where(keys[m] == c * LANES, spike[m], 0.0)
                k = c % per_x
                dsc[c // per_x, at_all, k * LANES:(k + 1) * LANES] = d.astype(jnp.bfloat16)

        part = jnp.zeros((rows, width), jnp.float32)
        block = pl.ds(pl.multiple_of(r * rows, rows), rows)
        for x in range(nx):
            part = part + jnp.dot(
                dsc[x, block, :], g_ref[x * cols_x:(x + 1) * cols_x, :],
                preferred_element_type=jnp.float32)

        @pl.when(first)
        def _():
            qp_out[zo] = part.astype(jnp.bfloat16)
            fold_copy(zo).start()

        @pl.when(jnp.logical_not(first))
        def _():
            own_part[zo] = part

            @pl.when(step > 0)
            def _():
                zf = lax.rem(z + step, depth)
                fold_copy(zf).wait_recv()
                z_out[step] = (own_part[zf] + qp_in[zf].astype(jnp.float32)).astype(jnp.bfloat16)
                home_copy(step).start()

    def pair_copy(x):
        return pltpu.make_async_remote_copy(
            src_ref=gal_b.at[x, 1 - core], dst_ref=ga_in.at[x], send_sem=ga_send.at[x], recv_sem=ga_recv.at[x],
            device_id={"pb": partner}, device_id_type=MESH)

    def chip_copy(k):
        return pltpu.make_async_remote_copy(
            src_ref=gb_out.at[k], dst_ref=gb_in.at[k], send_sem=gb_send.at[k], recv_sem=gb_recv.at[k],
            device_id={"pb": lax.rem(my_x + 1 + k, nx) * 2 + core}, device_id_type=MESH)

    qall = qs[...].reshape(n * rows, width)
    for k in range(nx):
        x = lax.rem(my_x + 1 + k, nx)
        for h in range(2):
            res = lax.dot_general(
                dsc[x, :, h * half:(h + 1) * half], qall, (((0,), (0,)), ((), ())),
                preferred_element_type=jnp.float32)
            gal_f[x, h] = res
            gal_b[x, h] = res.astype(jnp.bfloat16)
        pair_copy(x).start()

    for k in range(nx - 1):
        x = lax.rem(my_x + 1 + k, nx)
        pair_copy(x).wait_recv()
        gb_out[k] = (gal_f[x, core] + ga_in[x].astype(jnp.float32)).astype(jnp.bfloat16)
        chip_copy(k).start()
    pair_copy(my_x).wait_recv()
    gout_ref[...] = gal_f[my_x, core] + ga_in[my_x].astype(jnp.float32)

    fold_copy(z).wait_recv()
    qout_ref[...] = own_part[z] + qp_in[z].astype(jnp.float32)

    @pl.loop(1, depth)
    def _(k):
        home_copy(k).wait()
        qout_ref[...] += z_in[k].astype(jnp.float32)

    @pl.loop(0, depth)
    def _(k):
        fold_copy(k).wait_send()

    @pl.loop(0, 2 * (2 * depth - 1))
    def _(j):
        zo, yo, valid = candidate(j)

        @pl.when(valid)
        def _():
            for h in range(2):
                hops(zo, yo, h, lambda c: c.wait_send())

    for k in range(nx - 1):
        chip_copy(k).wait()
        gout_ref[...] += gb_in[k].astype(jnp.float32)

    @pl.loop(0, n)
    def _(r):
        exchange_wait(pos_in, r, pos_send, pos_recv).wait_send()
        exchange_wait(rank_in, r, rank_send, rank_recv).wait_send()

    @pl.loop(0, nx)
    def _(x):
        pair_copy(x).wait_send()


def shards(n, npb, queries, gallery, positives, cutoffs):
    rows, width = queries.shape
    gal = gallery.shape[0]
    members = positives.shape[1]
    nx = npb // 2
    half = gal // npb
    dma = pltpu.SemaphoreType.DMA
    vmem = pl.BlockSpec(memory_space=pltpu.VMEM)
    f32, bf16 = jnp.float32, jnp.bfloat16
    return pl.pallas_call(
        functools.partial(kernel, n, npb),
        out_shape=(
            jax.ShapeDtypeStruct((rows, width), f32),
            jax.ShapeDtypeStruct((half, width), f32),
        ),
        in_specs=[pl.BlockSpec(memory_space=pltpu.SMEM), vmem, vmem, vmem],
        out_specs=(vmem, vmem),
        scratch_shapes=[
            pltpu.VMEM((n, rows, width), bf16),
            pltpu.VMEM((n, rows, gal), f32),
            pltpu.VMEM((nx, n * rows, gal // nx), bf16),
            pltpu.VMEM((n, n, members, rows), f32),
            pltpu.VMEM((n, n, 2 * members, rows), f32),
            pltpu.VMEM((rows, LANES), f32),
            pltpu.VMEM((n, 2, rows, 8), f32),
            pltpu.VMEM((n // 2, rows, width), bf16),
            pltpu.VMEM((n // 2, rows, width), bf16),
            pltpu.VMEM((n // 2, rows, width), f32),
            pltpu.VMEM((n // 2, rows, width), bf16),
            pltpu.VMEM((n // 2, rows, width), bf16),
            pltpu.VMEM((nx, 2, half, width), f32),
            pltpu.VMEM((nx, 2, half, width), bf16),
            pltpu.VMEM((nx, half, width), bf16),
            pltpu.VMEM((max(nx - 1, 1), half, width), bf16),
            pltpu.VMEM((max(nx - 1, 1), half, width), bf16),
            dma((n, 2, 3)), dma((n, 2)), dma((n,)), dma((n,)), dma((n,)), dma((n,)),
            dma((n // 2,)), dma((n // 2,)), dma((n // 2,)), dma((n // 2,)),
            dma((nx,)), dma((nx,)), dma((nx,)), dma((nx,)),
        ],
        compiler_params=pltpu.CompilerParams(
            collective_id=0, has_side_effects=True, vmem_limit_bytes=62 * 1024 * 1024),
    )(cutoffs, queries, gallery, positives)


def solution(mesh):
    placed = (P(("pb", "ga"), None), P("ga", None), P("pb", None), P())
    return jax.shard_map(
        functools.partial(shards, mesh.shape["ga"], mesh.shape["pb"]),
        mesh=mesh,
        in_specs=placed,
        out_specs=(P(("pb", "ga"), None), P(("ga", "pb"), None)),
        check_vma=False,
    )
```
